32 devices in a mesh: col: 8 (over z, y), row: 4 (over x, core).
Axes of the slice: x: 2, y: 2, z: 4, core: 2. Of those that a mesh axis runs over, the one named last changes fastest.
Arguments:
- factor: float32 [8, 512, 1024], P('col', 'row'), may hold values from -0.6 to 0.6
- pattern: int32 [8, 4, 8], replicated, may hold values from 0 to 1, as said below
- order: int32 [8], replicated, may hold values from 0 to 7, each once
- targets: int32 [2, 2], replicated, may hold values from 0 to 3, as said below
- panels: float32 [512, 512], P('row'), may hold values from -6 to 6
Outputs:
- carried: float32 [8, 512, 512], P('col', 'row')
The draws below stay inside these ranges and needn't reach their ends.
Inputs may be any that keep to these rules, and one draw needn't show every extreme that they name: `pattern`: 0 or 1 for each block of a supernode's rows and factored columns; the share of present blocks differs between supernodes. `targets`: every row block 0..3 is named at least once.
All inputs are finite; a program needn't handle non-finite values.
Results may differ from the reference program's by a relative error of at most 0.0001.
Values sent between devices are 32-bit elements; how exact they have to be, the bound alone decides.
No kernel may reach another device: no remote copies, remote signals or barrier semaphores. Data moves between devices by JAX's collectives and lax.ppermute only.
A program may use at most 128 MiB of HBM per device.

```python
import jax
import jax.numpy as jnp
from jax import lax

BLOCK = 128
F = 1024
PANEL = 256
NP = 2
R_DEV = 128
ROWS = 512
N_COL = 8


def draw_pattern(key, part):
    first_key, second_key = jax.random.split(key)
    shares = jax.random.randint(first_key, (N_COL, 1, 1), 3, 8)
    cells = jax.random.randint(second_key, (N_COL, ROWS // BLOCK, F // BLOCK), 0, 10)
    return (cells < shares).astype(jnp.int32)


def draw_targets(key, part):
    slots = NP * (PANEL // BLOCK)
    owners = ROWS // R_DEV
    per_owner = R_DEV // BLOCK
    shuffled = jax.random.permutation(jax.random.fold_in(key, 3), slots)
    within = jax.random.randint(jax.random.fold_in(key, 7), (slots,), 0, per_owner)
    owner_of = shuffled % owners
    slot_ids = jnp.arange(slots, dtype=jnp.int32)
    top_slot = jnp.argmax((owner_of == owners - 1).astype(jnp.int32))
    bottom_slot = slots - 1 - jnp.argmax(jnp.flip((owner_of == 0).astype(jnp.int32)))
    within = jnp.where(slot_ids == top_slot, per_owner - 1, within)
    within = jnp.where(slot_ids == bottom_slot, 0, within)
    chosen = owner_of * per_owner + within
    return chosen.reshape(NP, PANEL // BLOCK).astype(jnp.int32)


def block_levels(own_key, shape, pieces, least, largest):
    loudness = 1.0
    for dim, shards_of in pieces:
        draws = jax.random.uniform(jax.random.fold_in(jax.random.fold_in(own_key, 6), dim), (shards_of,), jnp.float32, least / len(pieces), largest / len(pieces))
        loudness = loudness * jnp.repeat(jnp.exp(draws), shape[dim] // shards_of).reshape((-1,) + (1,) * (len(shape) - 1 - dim))
    return loudness


def noise(rng, dims, width, reach, cuts=(), kind=jnp.bfloat16):
    loudness = block_levels(rng, dims, cuts, -0.22, 0.18) if cuts else 1.0
    result = jax.random.normal(rng, dims, jnp.float32) * width * loudness
    return jnp.minimum(jnp.maximum(result, -reach), reach).astype(kind)


def setup_inputs(seed: int = 0) -> dict:
    key_list = jax.random.split(jax.random.key(seed), 6)
    factor = noise(key_list[0], (N_COL, ROWS, F), 0.09, 0.6, ((0, 8), (1, 4)), jnp.float32)
    pattern = draw_pattern(jax.random.fold_in(key_list[5], 71), 0)
    order = jax.random.permutation(key_list[2], N_COL).astype(jnp.int32)
    targets = draw_targets(jax.random.fold_in(key_list[5], 71), 0)
    panels = noise(key_list[4], (ROWS, NP * PANEL), 1.0, 6.0, ((0, 4),), jnp.float32)
    return {"factor": factor, "pattern": pattern, "order": order, "targets": targets, "panels": panels}


def reference(factor, pattern, order, targets, panels):
    row_blocks = ROWS // BLOCK
    col_blocks = F // BLOCK

    def step(state, inputs):
        owner_rows, position = inputs
        supernode = order[position]
        present = pattern[supernode].astype(jnp.float32)
        masked = (owner_rows.reshape(row_blocks, BLOCK, col_blocks, BLOCK) * present[:, None, :, None]).reshape(ROWS, F)
        strips = jnp.take(masked.reshape(row_blocks, BLOCK, F), targets.reshape(-1), axis=0).reshape(NP * PANEL, F)
        update = lax.dot_general(masked, strips, (((1,), (1,)), ((), ())), precision=lax.Precision.HIGHEST, preferred_element_type=jnp.float32)
        state = state - update
        return state, state

    _, carried = lax.scan(step, panels, (factor, jnp.arange(N_COL, dtype=jnp.int32)))
    return carried
```

```python
import functools

import jax
import jax.numpy as jnp
from jax import lax
from jax.experimental import pallas as pl
from jax.experimental.pallas import tpu as pltpu
from jax.sharding import PartitionSpec as P

BLOCK = 128
PARAMS = pltpu.CompilerParams(vmem_limit_bytes=8 << 20)
NT = (((1,), (1,)), ((), ()))


def halves(value):
    high = value.astype(jnp.bfloat16)
    return high, (value - high.astype(jnp.float32)).astype(jnp.bfloat16)


def product(left, right):
    dot = functools.partial(lax.dot_general, dimension_numbers=NT, preferred_element_type=jnp.float32)
    return dot(left[0], right[0]) + (dot(left[0], right[1]) + dot(left[1], right[0]))


def masked(ref, present_ref, row):
    columns = ref.shape[1] // BLOCK
    parts = []
    for k in range(columns):
        keep = present_ref[row, k].astype(jnp.float32)
        parts.append(ref[:, k * BLOCK : (k + 1) * BLOCK] * keep)
    return jnp.concatenate(parts, axis=1)


def near_kernel(present_ref, own_ref, sibling_ref, out_ref):
    row = lax.axis_index("row")
    own = halves(masked(own_ref, present_ref, row))
    sibling = halves(masked(sibling_ref, present_ref, row ^ 1))
    out_ref[0] = product(own, own)
    out_ref[1] = product(own, sibling)


def far_kernel(present_ref, own_ref, sibling_ref, across_ref, after_ref, mine_ref, theirs_ref):
    del after_ref
    row = lax.axis_index("row")
    own = halves(masked(own_ref, present_ref, row))
    sibling = halves(masked(sibling_ref, present_ref, row ^ 1))
    across = halves(masked(across_ref, present_ref, row ^ 2))
    mine_ref[...] = product(own, across)
    theirs_ref[...] = product(sibling, across)


def finish_kernel(bit, targets_ref, panels_ref, near_ref, near_in_ref, far_ref, far_in_ref, out_ref):
    row = lax.axis_index("row")
    upper = (lax.axis_index("col") & bit) != 0
    per_panel = targets_ref.shape[1]
    sums = [(near_ref, near_in_ref, 0), (near_ref, near_in_ref, 1), (far_ref, far_in_ref, 0), (far_ref, far_in_ref, 1)]
    for slot in range(targets_ref.shape[0] * per_panel):
        place = targets_ref[slot // per_panel, slot % per_panel] ^ row
        columns = slice(slot * BLOCK, (slot + 1) * BLOCK)
        for j, (inclusive, incoming, k) in enumerate(sums):

            @pl.when(place == j)
            def _():
                earlier = jnp.where(upper, incoming[k], jnp.zeros_like(incoming[k]))
                out_ref[:, columns] = panels_ref[:, columns] - (inclusive[k] + earlier)


def swapped(value, axis, bit):
    return lax.ppermute(value, axis, [(i, i ^ bit) for i in range(lax.axis_size(axis))])


def scanned(update):
    place, size = lax.axis_index("col"), lax.axis_size("col")
    inclusive, total, bit, totals = update, update, 1, [update]
    while bit * 2 < size:
        other = swapped(total, "col", bit)
        inclusive = inclusive + jnp.where((place & bit) != 0, other, 0.0)
        total = total + other
        totals.append(total)
        bit *= 2
    return inclusive, swapped(total, "col", bit), bit, totals


def body(factor, pattern, order, targets, panels):
    own = factor[0]
    rows, width = own.shape
    smem, vmem = pl.BlockSpec(memory_space=pltpu.SMEM), pl.BlockSpec(memory_space=pltpu.VMEM)
    f32 = jnp.float32
    across = swapped(own, "row", 2)
    sibling = swapped(own, "row", 1)
    supernode = lax.dynamic_index_in_dim(order, lax.axis_index("col"), 0, keepdims=False)
    present = lax.dynamic_index_in_dim(pattern, supernode, 0, keepdims=False)
    flops = 2 * 3 * rows * BLOCK * width
    near = pl.pallas_call(
        near_kernel,
        out_shape=jax.ShapeDtypeStruct((2, rows, BLOCK), f32),
        in_specs=[smem, vmem, vmem],
        out_specs=vmem,
        compiler_params=PARAMS,
        cost_estimate=pl.CostEstimate(flops=2 * flops, bytes_accessed=8 * rows * width, transcendentals=0),
    )(present, own, sibling)
    near_sum, near_in, bit, totals = scanned(near)
    mine, theirs = pl.pallas_call(
        far_kernel,
        out_shape=[jax.ShapeDtypeStruct((rows, BLOCK), f32)] * 2,
        in_specs=[smem, vmem, vmem, vmem, pl.BlockSpec(memory_space=pl.ANY)],
        out_specs=[vmem, vmem],
        compiler_params=PARAMS,
        cost_estimate=pl.CostEstimate(flops=2 * flops, bytes_accessed=12 * rows * width, transcendentals=0),
    )(present, own, sibling, across, totals[1])
    far = jnp.stack([mine, swapped(theirs, "row", 1)])
    far_sum, far_in, bit, _ = scanned(far)
    carried = pl.pallas_call(
        functools.partial(finish_kernel, bit),
        out_shape=jax.ShapeDtypeStruct(panels.shape, f32),
        in_specs=[smem, vmem, vmem, vmem, vmem, vmem],
        out_specs=vmem,
        compiler_params=PARAMS,
        cost_estimate=pl.CostEstimate(flops=0, bytes_accessed=16 * rows * panels.shape[1], transcendentals=0),
    )(targets, panels, near_sum, near_in, far_sum, far_in)
    return carried[None]


def solution(mesh):
    placed = (P("col", "row", None), P(), P(), P(), P("row", None))
    return jax.shard_map(
        body, mesh=mesh, in_specs=placed, out_specs=P("col", "row", None), check_vma=False
    )
```

```python
import functools

import jax
import jax.numpy as jnp
from jax import lax
from jax.experimental import pallas as pl
from jax.experimental.pallas import tpu as pltpu
from jax.sharding import PartitionSpec as P


BLOCK = 128
PARAMS = pltpu.CompilerParams(vmem_limit_bytes=8 << 20)
NT = (((1,), (1,)), ((), ()))
SMEM = pl.BlockSpec(memory_space=pltpu.SMEM)
VMEM = pl.BlockSpec(memory_space=pltpu.VMEM)
F32, BF16 = jnp.float32, jnp.bfloat16


def halves(value):
    high = value.astype(BF16)
    return high, (value - high.astype(F32)).astype(BF16)


def product(left, right):
    dot = functools.partial(lax.dot_general, dimension_numbers=NT, preferred_element_type=F32)
    return dot(left[0], right[0]) + (dot(left[0], right[1]) + dot(left[1], right[0]))


def masked(ref, present_ref, row):
    parts = []
    for k in range(ref.shape[1] // BLOCK):
        keep = present_ref[row, k].astype(F32)
        parts.append(ref[:, k * BLOCK : (k + 1) * BLOCK] * keep)
    return jnp.concatenate(parts, axis=1)


def near_kernel(order_ref, pattern_ref, own_ref, sibling_ref, out_ref, high_ref, low_ref, present_ref):
    row = lax.axis_index("row")
    supernode = order_ref[lax.axis_index("col")]
    for i in range(pattern_ref.shape[1]):
        for k in range(pattern_ref.shape[2]):
            present_ref[i, k] = pattern_ref[supernode, i, k]
    own = halves(masked(own_ref, present_ref, row))
    sibling = halves(masked(sibling_ref, present_ref, row ^ 1))
    out_ref[0] = product(own, own)
    out_ref[1] = product(own, sibling)
    for kept, mine, theirs in zip((high_ref, low_ref), own, sibling, strict=True):
        kept[...] = jnp.where((row & 2) == 0, mine, theirs)


def far_kernel(present_ref, high_ref, low_ref, across_ref, out_ref):
    across = halves(masked(across_ref, present_ref, lax.axis_index("row") ^ 2))
    out_ref[...] = product(across, (high_ref[...], low_ref[...]))


def finish_kernel(bit, targets_ref, panels_ref, near_ref, near_in_ref, own_ref, across_ref, sibling_ref, out_ref):
    row = lax.axis_index("row")
    upper = (lax.axis_index("col") & bit) != 0
    first = (row & 2) == 0
    slots = range(targets_ref.shape[0] * targets_ref.shape[1])

    def place(j, value):
        for slot in slots:
            columns = slice(slot * BLOCK, (slot + 1) * BLOCK)

            @pl.when((targets_ref[slot // targets_ref.shape[1], slot % targets_ref.shape[1]] ^ row) == j)
            def _():
                out_ref[:, columns] = panels_ref[:, columns] - value

    for j in range(2):
        earlier = jnp.where(upper, near_in_ref[j], jnp.zeros_like(near_in_ref[j]))
        place(j, near_ref[j] + earlier)
    turned = jnp.where(first, own_ref[...], sibling_ref[...]).T
    straight = across_ref[...]
    place(2, jnp.where(first, turned, straight))
    place(3, jnp.where(first, straight, turned))


def swapped(value, axis, bit):
    return lax.ppermute(value, axis, [(i, i ^ bit) for i in range(lax.axis_size(axis))])


def scanned(update):
    place, size = lax.axis_index("col"), lax.axis_size("col")
    inclusive, total, bit = update, update, 1
    while bit * 2 < size:
        other = swapped(total, "col", bit)
        inclusive = inclusive + jnp.where((place & bit) != 0, other, 0.0)
        total = total + other
        bit = bit * 2
    return inclusive, swapped(total, "col", bit), bit


def kernel(call, **kwargs):
    def run(*args):
        return pl.pallas_call(call, compiler_params=PARAMS, **kwargs)(*args)

    return run


def body(factor, pattern, order, targets, panels):
    own = factor[0]
    rows, width = own.shape
    sibling = swapped(own, "row", 1)
    across = swapped(own, "row", 2)
    flops = 2 * 3 * rows * BLOCK * width
    near, high, low, present = kernel(
        near_kernel,
        out_shape=[
            jax.ShapeDtypeStruct((2, rows, BLOCK), F32),
            jax.ShapeDtypeStruct((rows, width), BF16),
            jax.ShapeDtypeStruct((rows, width), BF16),
            jax.ShapeDtypeStruct(pattern.shape[1:], jnp.int32),
        ],
        in_specs=[SMEM, SMEM, VMEM, VMEM],
        out_specs=[VMEM, VMEM, VMEM, SMEM],
        cost_estimate=pl.CostEstimate(flops=2 * flops, bytes_accessed=12 * rows * width, transcendentals=0),
    )(order, pattern, own, sibling)
    near_sum, near_in, bit = scanned(near)
    far = kernel(
        far_kernel,
        out_shape=jax.ShapeDtypeStruct((rows, rows), F32),
        in_specs=[SMEM, VMEM, VMEM, VMEM],
        out_specs=VMEM,
        cost_estimate=pl.CostEstimate(flops=flops, bytes_accessed=8 * rows * width, transcendentals=0),
    )(present, high, low, across)
    far_sum, far_in, bit = scanned(far)
    mine = far_sum + jnp.where((lax.axis_index("col") & bit) != 0, far_in, 0.0)
    theirs, beside = swapped(mine, "row", 2), swapped(mine, "row", 1)
    carried = kernel(
        functools.partial(finish_kernel, bit),
        out_shape=jax.ShapeDtypeStruct(panels.shape, F32),
        in_specs=[SMEM] + [VMEM] * 6,
        out_specs=VMEM,
        cost_estimate=pl.CostEstimate(flops=0, bytes_accessed=16 * rows * panels.shape[1], transcendentals=0),
    )(targets, panels, near_sum, near_in, mine, theirs, beside)
    return carried[None]


def solution(mesh):
    placed = (P("col", "row", None), P(), P(), P(), P("row", None))
    return jax.shard_map(
        body, mesh=mesh, in_specs=placed, out_specs=P("col", "row", None), check_vma=False
    )
```

```python
import functools

import jax
import jax.numpy as jnp
from jax import lax
from jax.experimental import pallas as pl
from jax.experimental.pallas import tpu as pltpu
from jax.sharding import PartitionSpec as P


BLOCK = 128
HALF = BLOCK // 2
PARAMS = pltpu.CompilerParams(vmem_limit_bytes=8 << 20)
NT = (((1,), (1,)), ((), ()))
SMEM = pl.BlockSpec(memory_space=pltpu.SMEM)
VMEM = pl.BlockSpec(memory_space=pltpu.VMEM)
ANY = pl.BlockSpec(memory_space=pl.ANY)
HBM = pl.BlockSpec(memory_space=pltpu.HBM)
F32, BF16 = jnp.float32, jnp.bfloat16


def odd(place, bits):
    parity = place & 1
    for k in range(1, bits):
        parity ^= (place >> k) & 1
    return parity


def halves(value):
    high = value.astype(BF16)
    return high, (value - high.astype(F32)).astype(BF16)


def product(left, right):
    dot = functools.partial(lax.dot_general, dimension_numbers=NT, preferred_element_type=F32)
    return dot(left[0], right[0]) + (dot(left[0], right[1]) + dot(left[1], right[0]))


def masked(ref, present_ref, row):
    parts = []
    for k in range(ref.shape[1] // BLOCK):
        keep = present_ref[row, k].astype(F32)
        parts.append(ref[:, k * BLOCK : (k + 1) * BLOCK] * keep)
    return jnp.concatenate(parts, axis=1)


def left_lanes(shape):
    return lax.broadcasted_iota(jnp.int32, shape, 1) < HALF


def near_kernel(bits, order_ref, pattern_ref, own_hbm, sibling_ref, out_ref, high_ref, low_ref, present_ref, own_ref, sems):
    row, place = lax.axis_index("row"), lax.axis_index("col")
    rows = pltpu.make_async_copy(own_hbm, own_ref, sems.at[0])
    rows.start()
    cells = pltpu.make_async_copy(pattern_ref.at[order_ref[place]], present_ref, sems.at[1])
    cells.start()
    cells.wait()
    sibling = halves(masked(sibling_ref, present_ref, row ^ 1))
    rows.wait()
    own = halves(masked(own_ref, present_ref, row))
    diagonal = product(own, own)
    out_ref[0:HALF] = diagonal[0:HALF]
    corner, quarter = diagonal[HALF:], HALF // 2
    moved = pltpu.roll(corner[0:quarter], HALF, axis=1)
    out_ref[HALF : HALF + quarter] = jnp.where(left_lanes(moved.shape), moved, corner[quarter:])
    first = (row & 1) == 0
    shared = product(
        [jnp.where(first, a[0:HALF], b[HALF:]) for a, b in zip(own, sibling, strict=True)],
        [jnp.where(first, b, a) for a, b in zip(own, sibling, strict=True)],
    )
    out_ref[HALF + quarter :] = shared
    plain = (((row >> 1) & 1) ^ odd(place, bits)) == 0
    for kept, mine, theirs in zip((high_ref, low_ref), own, sibling, strict=True):
        kept[...] = jnp.where(plain, mine, theirs)


def far_kernel(bits, present_ref, high_ref, low_ref, across_ref, out_ref):
    row = lax.axis_index("row") ^ odd(lax.axis_index("col"), bits)
    across = halves(masked(across_ref, present_ref, row ^ 2))
    out_ref[...] = product(across, (high_ref[...], low_ref[...]))


def columns_of(j, targets_ref, slot):
    return (targets_ref[slot // targets_ref.shape[1], slot % targets_ref.shape[1]] ^ lax.axis_index("row")) == j


def write(values, targets_ref, panels_ref, out_hbm, staged_ref, sems):
    slots = range(targets_ref.shape[0] * targets_ref.shape[1])
    for wait in (False, True):
        for j, value in values.items():
            for slot in slots:
                columns = slice(slot * BLOCK, (slot + 1) * BLOCK)
                copy = pltpu.make_async_copy(staged_ref.at[slot], out_hbm.at[:, columns], sems.at[slot])

                @pl.when(columns_of(j, targets_ref, slot))
                def _():
                    if wait:
                        copy.wait()
                    else:
                        staged_ref[slot] = panels_ref[:, columns] - value
                        copy.start()


def near_finish_kernel(targets_ref, panels_ref, near_ref, beside_ref, out_hbm, staged_ref, sems):
    quarter = HALF // 2
    upper = near_ref[0:HALF]
    turned = jnp.concatenate([upper, upper]).T[HALF:]
    corner = near_ref[HALF : HALF + quarter]
    corner = jnp.concatenate([pltpu.roll(corner, HALF, axis=1), corner])
    diagonal = jnp.concatenate([upper, jnp.where(left_lanes(corner.shape), turned, corner)])
    first = (lax.axis_index("row") & 1) == 0
    mine, theirs = near_ref[HALF + quarter :], beside_ref[...]
    shared = jnp.concatenate([jnp.where(first, mine, theirs), jnp.where(first, theirs, mine)])
    shared = jnp.where(first, shared, shared.T)
    write({0: diagonal, 1: shared}, targets_ref, panels_ref, out_hbm, staged_ref, sems)


def far_finish_kernel(bits, targets_ref, panels_ref, own_ref, across_ref, beside_ref, begun_hbm, out_hbm, staged_ref, sems):
    del begun_hbm
    second = (lax.axis_index("row") >> 1) & 1
    plain = (second ^ odd(lax.axis_index("col"), bits)) == 0
    turned = jnp.where(plain, own_ref[...], beside_ref[...]).T
    straight, first = across_ref[...], second == 0
    write(
        {2: jnp.where(first, turned, straight), 3: jnp.where(first, straight, turned)},
        targets_ref,
        panels_ref,
        out_hbm,
        staged_ref,
        sems,
    )


def moved(value, to):
    columns, rows = lax.axis_size("col"), lax.axis_size("row")
    pairs = []
    for place in range(columns):
        for row in range(rows):
            there, other = to(place, row)
            pairs.append((place * rows + row, there * rows + other))
    return lax.ppermute(value, ("col", "row"), pairs)


def scanned(update, turn):
    place, size = lax.axis_index("col"), lax.axis_size("col")
    inclusive, total, bit = update, update, 1
    while bit < size:
        other = moved(total, lambda p, r, bit=bit: (p ^ bit, r ^ turn))
        inclusive = inclusive + jnp.where((place & bit) != 0, other, 0.0)
        total = total + other
        bit = bit * 2
    return inclusive


def kernel(call, **kwargs):
    def run(*args):
        return pl.pallas_call(call, compiler_params=PARAMS, **kwargs)(*args)

    return run


def body(factor, pattern, order, targets, panels):
    own = factor[0]
    rows, width = own.shape
    bits = (lax.axis_size("col") - 1).bit_length()
    cost = functools.partial(pl.CostEstimate, transcendentals=0)
    flops = 2 * 3 * rows * BLOCK * width
    sibling = moved(own, lambda p, r: (p, r ^ 1))
    across = moved(own, lambda p, r: (p, r ^ 2 ^ odd(p, bits)))
    near, high, low, present = kernel(
        functools.partial(near_kernel, bits),
        out_shape=[
            jax.ShapeDtypeStruct((BLOCK + HALF // 2, BLOCK), F32),
            jax.ShapeDtypeStruct((rows, width), BF16),
            jax.ShapeDtypeStruct((rows, width), BF16),
            jax.ShapeDtypeStruct(pattern.shape[1:], jnp.int32),
        ],
        in_specs=[SMEM, HBM, HBM, VMEM],
        out_specs=[VMEM, VMEM, VMEM, SMEM],
        scratch_shapes=[pltpu.VMEM((rows, width), F32), pltpu.SemaphoreType.DMA((2,))],
        cost_estimate=cost(flops=2 * flops, bytes_accessed=12 * rows * width),
    )(order, pattern, own, sibling)
    near_sum = scanned(near, 0)
    far = kernel(
        functools.partial(far_kernel, bits),
        out_shape=jax.ShapeDtypeStruct((rows, rows), F32),
        in_specs=[SMEM, VMEM, VMEM, VMEM],
        out_specs=VMEM,
        cost_estimate=cost(flops=flops, bytes_accessed=8 * rows * width),
    )(present, high, low, across)
    far_sum = scanned(far, 1)
    shared = moved(near_sum[HALF + HALF // 2 :], lambda p, r: (p, r ^ 1))
    theirs = moved(far_sum, lambda p, r: (p, r ^ 2 ^ odd(p, bits)))
    beside = moved(far_sum, lambda p, r: (p, r ^ 1))
    slots = targets.shape[0] * targets.shape[1]
    writing = dict(
        out_shape=jax.ShapeDtypeStruct(panels.shape, F32),
        out_specs=ANY,
        scratch_shapes=[pltpu.VMEM((slots, rows, BLOCK), F32), pltpu.SemaphoreType.DMA((slots,))],
        cost_estimate=cost(flops=0, bytes_accessed=12 * rows * panels.shape[1]),
    )
    begun = kernel(near_finish_kernel, in_specs=[SMEM] + [VMEM] * 3, **writing)(targets, panels, near_sum, shared)
    carried = kernel(
        functools.partial(far_finish_kernel, bits),
        in_specs=[SMEM] + [VMEM] * 4 + [ANY],
        input_output_aliases={5: 0},
        **writing,
    )(targets, panels, far_sum, theirs, beside, begun)
    return carried[None]


def solution(mesh):
    placed = (P("col", "row", None), P(), P(), P(), P("row", None))
    return jax.shard_map(
        body, mesh=mesh, in_specs=placed, out_specs=P("col", "row", None), check_vma=False
    )
```

```python
import functools

import jax
import jax.numpy as jnp
from jax import lax
from jax.experimental import pallas as pl
from jax.experimental.pallas import tpu as pltpu
from jax.sharding import PartitionSpec as P


BLOCK = 128
HALF = BLOCK // 2
PARAMS = pltpu.CompilerParams(vmem_limit_bytes=8 << 20)
NT = (((1,), (1,)), ((), ()))
SMEM = pl.BlockSpec(memory_space=pltpu.SMEM)
VMEM = pl.BlockSpec(memory_space=pltpu.VMEM)
ANY = pl.BlockSpec(memory_space=pl.ANY)
F32, BF16 = jnp.float32, jnp.bfloat16


def odd(place, bits):
    parity = place & 1
    for k in range(1, bits):
        parity ^= (place >> k) & 1
    return parity


def halves(value):
    high = value.astype(BF16)
    return high, (value - high.astype(F32)).astype(BF16)


def product(left, right):
    dot = functools.partial(lax.dot_general, dimension_numbers=NT, preferred_element_type=F32)
    return dot(left[0], right[0]) + (dot(left[0], right[1]) + dot(left[1], right[0]))


def left_lanes(shape):
    return lax.broadcasted_iota(jnp.int32, shape, 1) < HALF


def split_kernel(rows_ref, high_ref, low_ref):
    high_ref[...], low_ref[...] = halves(rows_ref[...])


def near_kernel(bits, order_ref, pattern_ref, high_ref, low_ref, sibling_ref, out_ref, left_high_ref, left_low_ref, mask_ref):
    row, place = lax.axis_index("row"), lax.axis_index("col")
    supernode, parity = order_ref[place], odd(place, bits)

    def masked(parts, block):
        kept = ([], [])
        for k in range(parts[0].shape[1] // BLOCK):
            present = pattern_ref[supernode, block, k] != 0
            for part, out in zip(parts, kept, strict=True):
                piece = part[:, k * BLOCK : (k + 1) * BLOCK]
                out.append(jnp.where(present, piece, jnp.zeros_like(piece)))
        return [jnp.concatenate(out, axis=1) for out in kept]

    own = masked((high_ref[...], low_ref[...]), row)
    sibling = masked(halves(sibling_ref[...]), row ^ 1)
    diagonal = product(own, own)
    out_ref[0:HALF] = diagonal[0:HALF]
    corner, quarter = diagonal[HALF:], HALF // 2
    turned = pltpu.roll(corner[0:quarter], HALF, axis=1)
    out_ref[HALF : HALF + quarter] = jnp.where(left_lanes(turned.shape), turned, corner[quarter:])
    first = (row & 1) == 0
    shared = product(
        [jnp.where(first, a[0:HALF], b[HALF:]) for a, b in zip(own, sibling, strict=True)],
        [jnp.where(first, b, a) for a, b in zip(own, sibling, strict=True)],
    )
    out_ref[HALF + quarter :] = shared
    plain = (((row >> 1) & 1) ^ parity) == 0
    for kept, mine, theirs in zip((left_high_ref, left_low_ref), own, sibling, strict=True):
        kept[...] = jnp.where(plain, mine, theirs)
    for k in range(mask_ref.shape[1] // BLOCK):
        keep = pattern_ref[supernode, row ^ parity ^ 2, k].astype(F32)
        mask_ref[:, k * BLOCK : (k + 1) * BLOCK] = jnp.full((mask_ref.shape[0], BLOCK), keep)


def far_kernel(mask_ref, high_ref, low_ref, across_ref, out_ref):
    across = halves(across_ref[...] * mask_ref[0:1])
    out_ref[...] = product(across, (high_ref[...], low_ref[...]))


def near_finish_kernel(targets_ref, panels_ref, near_ref, beside_ref, out_ref, which_ref):
    quarter = HALF // 2
    upper = near_ref[0:HALF]
    turned = jnp.concatenate([upper, upper]).T[HALF:]
    corner = near_ref[HALF : HALF + quarter]
    corner = jnp.concatenate([pltpu.roll(corner, HALF, axis=1), corner])
    diagonal = jnp.concatenate([upper, jnp.where(left_lanes(corner.shape), turned, corner)])
    row, per_panel = lax.axis_index("row"), targets_ref.shape[1]
    first = (row & 1) == 0
    mine, theirs = near_ref[HALF + quarter :], beside_ref[...]
    shared = jnp.concatenate([jnp.where(first, mine, theirs), jnp.where(first, theirs, mine)])
    shared = jnp.where(first, shared, shared.T)
    for slot in range(targets_ref.shape[0] * per_panel):
        columns = slice(slot * BLOCK, (slot + 1) * BLOCK)
        j = targets_ref[slot // per_panel, slot % per_panel] ^ row
        near = jnp.where(j == 0, diagonal, jnp.where(j == 1, shared, jnp.zeros_like(shared)))
        out_ref[:, columns] = panels_ref[:, columns] - near
        which_ref[:, columns] = jnp.full((which_ref.shape[0], BLOCK), j)


def far_finish_kernel(bits, which_ref, begun_ref, own_ref, across_ref, beside_ref, out_hbm, staged_ref, sems):
    second = (lax.axis_index("row") >> 1) & 1
    plain, first = (second ^ odd(lax.axis_index("col"), bits)) == 0, second == 0
    turned, straight = jnp.where(plain, own_ref[...], beside_ref[...]).T, across_ref[...]
    two, three = jnp.where(first, turned, straight), jnp.where(first, straight, turned)
    copies = []
    for slot in range(staged_ref.shape[0]):
        columns = slice(slot * BLOCK, (slot + 1) * BLOCK)
        j = which_ref[0:1, columns]
        far = jnp.where(j == 2, two, jnp.where(j == 3, three, 0.0))
        staged_ref[slot] = begun_ref[:, columns] - far
        copies.append(pltpu.make_async_copy(staged_ref.at[slot], out_hbm.at[:, columns], sems.at[slot]))
        copies[-1].start()
    for copy in copies:
        copy.wait()


def moved(value, to):
    columns, rows = lax.axis_size("col"), lax.axis_size("row")
    pairs = []
    for place in range(columns):
        for row in range(rows):
            there, other = to(place, row)
            pairs.append((place * rows + row, there * rows + other))
    return lax.ppermute(value, ("col", "row"), pairs)


def scanned(update, turn):
    place, size = lax.axis_index("col"), lax.axis_size("col")
    inclusive, total, bit = update, update, 1
    while bit < size:
        other = moved(total, lambda p, r, bit=bit: (p ^ bit, r ^ turn))
        inclusive = inclusive + jnp.where((place & bit) != 0, other, 0.0)
        total = total + other
        bit = bit * 2
    return inclusive


def kernel(call, **kwargs):
    def run(*args):
        return pl.pallas_call(call, compiler_params=PARAMS, **kwargs)(*args)

    return run


def body(factor, pattern, order, targets, panels):
    own = factor[0]
    rows, width = own.shape
    bits = (lax.axis_size("col") - 1).bit_length()
    cost = functools.partial(pl.CostEstimate, transcendentals=0)
    flops = 2 * 3 * rows * BLOCK * width
    across = moved(own, lambda p, r: (p, r ^ 2 ^ odd(p, bits)))
    sibling = moved(own, lambda p, r: (p, r ^ 1))
    pair = [jax.ShapeDtypeStruct((rows, width), BF16)] * 2
    high, low = kernel(
        split_kernel,
        out_shape=pair,
        in_specs=[VMEM],
        out_specs=[VMEM] * 2,
        cost_estimate=cost(flops=4 * rows * width, bytes_accessed=8 * rows * width),
    )(own)
    near, high, low, mask = kernel(
        functools.partial(near_kernel, bits),
        out_shape=[jax.ShapeDtypeStruct((BLOCK + HALF // 2, BLOCK), F32), *pair, jax.ShapeDtypeStruct((8, width), F32)],
        in_specs=[SMEM] * 2 + [VMEM] * 3,
        out_specs=[VMEM] * 4,
        cost_estimate=cost(flops=2 * flops, bytes_accessed=12 * rows * width),
    )(order, pattern, high, low, sibling)
    near_sum = scanned(near, 0)
    far = kernel(
        far_kernel,
        out_shape=jax.ShapeDtypeStruct((rows, rows), F32),
        in_specs=[VMEM] * 4,
        out_specs=VMEM,
        cost_estimate=cost(flops=flops, bytes_accessed=8 * rows * width),
    )(mask, high, low, across)
    far_sum = scanned(far, 1)
    shared = moved(near_sum[HALF + HALF // 2 :], lambda p, r: (p, r ^ 1))
    theirs = moved(far_sum, lambda p, r: (p, r ^ 2 ^ odd(p, bits)))
    beside = moved(far_sum, lambda p, r: (p, r ^ 1))
    slots = targets.shape[0] * targets.shape[1]
    writing = cost(flops=0, bytes_accessed=12 * rows * panels.shape[1])
    begun, which = kernel(
        near_finish_kernel,
        out_shape=[jax.ShapeDtypeStruct(panels.shape, F32), jax.ShapeDtypeStruct((8, panels.shape[1]), jnp.int32)],
        in_specs=[SMEM] + [VMEM] * 3,
        out_specs=[VMEM] * 2,
        cost_estimate=writing,
    )(targets, panels, near_sum, shared)
    carried = kernel(
        functools.partial(far_finish_kernel, bits),
        out_shape=jax.ShapeDtypeStruct(panels.shape, F32),
        in_specs=[VMEM] * 5,
        out_specs=ANY,
        scratch_shapes=[pltpu.VMEM((slots, rows, BLOCK), F32), pltpu.SemaphoreType.DMA((slots,))],
        cost_estimate=writing,
    )(which, begun, far_sum, theirs, beside)
    return carried[None]


def solution(mesh):
    placed = (P("col", "row", None), P(), P(), P(), P("row", None))
    return jax.shard_map(
        body, mesh=mesh, in_specs=placed, out_specs=P("col", "row", None), check_vma=False
    )
```

```python
import functools

import jax
import jax.numpy as jnp
from jax import lax
from jax.experimental import pallas as pl
from jax.experimental.pallas import tpu as pltpu
from jax.sharding import PartitionSpec as P


BLOCK = 128
HALF = BLOCK // 2
PARAMS = pltpu.CompilerParams(vmem_limit_bytes=8 << 20)
NT = (((1,), (1,)), ((), ()))
SMEM = pl.BlockSpec(memory_space=pltpu.SMEM)
VMEM = pl.BlockSpec(memory_space=pltpu.VMEM)
HBM = pl.BlockSpec(memory_space=pltpu.HBM)
ANY = pl.BlockSpec(memory_space=pl.ANY)
F32, BF16 = jnp.float32, jnp.bfloat16


def odd(place, bits):
    parity = place & 1
    for k in range(1, bits):
        parity ^= (place >> k) & 1
    return parity


def halves(value):
    high = value.astype(BF16)
    return high, (value - high.astype(F32)).astype(BF16)


def product(left, right):
    dot = functools.partial(lax.dot_general, dimension_numbers=NT, preferred_element_type=F32)
    return dot(left[0], right[0]) + (dot(left[0], right[1]) + dot(left[1], right[0]))


def left_lanes(shape):
    return lax.broadcasted_iota(jnp.int32, shape, 1) < HALF


def split_kernel(bits, order_hbm, pattern_hbm, rows_hbm, high_ref, low_ref, masks_ref, order_ref, cells_ref, rows_ref, sems):
    row, place = lax.axis_index("row"), lax.axis_index("col")
    rows = pltpu.make_async_copy(rows_hbm, rows_ref, sems.at[0])
    rows.start()
    known = pltpu.make_async_copy(order_hbm, order_ref, sems.at[1])
    known.start()
    known.wait()
    cells = pltpu.make_async_copy(pattern_hbm.at[order_ref[place]], cells_ref, sems.at[2])
    cells.start()
    cells.wait()
    for n, block in enumerate((row ^ 1, row ^ odd(place, bits) ^ 2)):
        for k in range(masks_ref.shape[2] // BLOCK):
            keep = jnp.full(masks_ref.shape[1:2] + (BLOCK,), cells_ref[block, k].astype(F32))
            masks_ref[n, :, k * BLOCK : (k + 1) * BLOCK] = keep
    rows.wait()
    for k in range(rows_ref.shape[1] // BLOCK):
        columns = slice(k * BLOCK, (k + 1) * BLOCK)
        high_ref[:, columns], low_ref[:, columns] = halves(rows_ref[:, columns] * cells_ref[row, k].astype(F32))


def near_kernel(bits, masks_ref, high_ref, low_ref, sibling_ref, out_ref, left_high_ref, left_low_ref):
    row = lax.axis_index("row")
    own = (high_ref[...], low_ref[...])
    sibling = halves(sibling_ref[...] * masks_ref[0, 0:1])
    diagonal = product(own, own)
    out_ref[0:HALF] = diagonal[0:HALF]
    corner, quarter = diagonal[HALF:], HALF // 2
    turned = pltpu.roll(corner[0:quarter], HALF, axis=1)
    out_ref[HALF : HALF + quarter] = jnp.where(left_lanes(turned.shape), turned, corner[quarter:])
    first = (row & 1) == 0
    out_ref[HALF + quarter :] = product(
        [jnp.where(first, a[0:HALF], b[HALF:]) for a, b in zip(own, sibling, strict=True)],
        [jnp.where(first, b, a) for a, b in zip(own, sibling, strict=True)],
    )
    plain = (((row >> 1) & 1) ^ odd(lax.axis_index("col"), bits)) == 0
    for kept, mine, theirs in zip((left_high_ref, left_low_ref), own, sibling, strict=True):
        kept[...] = jnp.where(plain, mine, theirs)


def far_kernel(masks_ref, high_ref, low_ref, across_ref, out_ref):
    across = halves(across_ref[...] * masks_ref[1, 0:1])
    out_ref[...] = product(across, (high_ref[...], low_ref[...]))


def near_finish_kernel(targets_ref, panels_ref, near_ref, beside_ref, out_ref, which_ref):
    quarter = HALF // 2
    upper = near_ref[0:HALF]
    turned = jnp.concatenate([upper, upper]).T[HALF:]
    corner = near_ref[HALF : HALF + quarter]
    corner = jnp.concatenate([pltpu.roll(corner, HALF, axis=1), corner])
    diagonal = jnp.concatenate([upper, jnp.where(left_lanes(corner.shape), turned, corner)])
    row, per_panel = lax.axis_index("row"), targets_ref.shape[1]
    first = (row & 1) == 0
    mine, theirs = near_ref[HALF + quarter :], beside_ref[...]
    shared = jnp.concatenate([jnp.where(first, mine, theirs), jnp.where(first, theirs, mine)])
    shared = jnp.where(first, shared, shared.T)
    for slot in range(targets_ref.shape[0] * per_panel):
        columns = slice(slot * BLOCK, (slot + 1) * BLOCK)
        j = targets_ref[slot // per_panel, slot % per_panel] ^ row
        near = jnp.where(j == 0, diagonal, jnp.where(j == 1, shared, jnp.zeros_like(shared)))
        out_ref[:, columns] = panels_ref[:, columns] - near
        which_ref[:, columns] = jnp.full((which_ref.shape[0], BLOCK), j)


def far_finish_kernel(bits, which_ref, begun_ref, own_ref, across_ref, beside_ref, out_hbm, staged_ref, sems):
    second = (lax.axis_index("row") >> 1) & 1
    plain, first = (second ^ odd(lax.axis_index("col"), bits)) == 0, second == 0
    turned, straight = jnp.where(plain, own_ref[...], beside_ref[...]).T, across_ref[...]
    two, three = jnp.where(first, turned, straight), jnp.where(first, straight, turned)
    copies = []
    for slot in range(staged_ref.shape[0]):
        columns = slice(slot * BLOCK, (slot + 1) * BLOCK)
        j = which_ref[0:1, columns]
        far = jnp.where(j == 2, two, jnp.where(j == 3, three, 0.0))
        staged_ref[slot] = begun_ref[:, columns] - far
        copies.append(pltpu.make_async_copy(staged_ref.at[slot], out_hbm.at[:, columns], sems.at[slot]))
        copies[-1].start()
    for copy in copies:
        copy.wait()


def moved(value, to):
    columns, rows = lax.axis_size("col"), lax.axis_size("row")
    pairs = []
    for place in range(columns):
        for row in range(rows):
            there, other = to(place, row)
            pairs.append((place * rows + row, there * rows + other))
    return lax.ppermute(value, ("col", "row"), pairs)


def steps_of(size):
    low, steps = 1, []
    while low < size:
        steps.append((low, min(4, size // low)))
        low *= steps[-1][1]
    return steps


def scanned(update, turn):
    place = lax.axis_index("col")
    inclusive, total = update, update
    for low, count in steps_of(lax.axis_size("col")):
        others = {
            flip: moved(total, lambda p, r, flip=flip: (p ^ low * flip, r ^ turn * odd(flip, 2)))
            for flip in reversed(range(1, count))
        }
        digit = (place // low) % count
        inclusive = inclusive + sum(jnp.where((digit ^ flip) < digit, other, 0.0) for flip, other in others.items())
        total = total + sum(others.values())
    return inclusive


def kernel(call, **kwargs):
    def run(*args):
        return pl.pallas_call(call, compiler_params=PARAMS, **kwargs)(*args)

    return run


def body(factor, pattern, order, targets, panels):
    own = factor[0]
    rows, width = own.shape
    bits = (lax.axis_size("col") - 1).bit_length()
    cost = functools.partial(pl.CostEstimate, transcendentals=0)
    flops = 2 * 3 * rows * BLOCK * width
    across = moved(own, lambda p, r: (p, r ^ 2 ^ odd(p, bits)))
    sibling = moved(own, lambda p, r: (p, r ^ 1))
    pair = [jax.ShapeDtypeStruct((rows, width), BF16)] * 2
    held = functools.partial(pltpu.with_memory_space_constraint, memory_space=pltpu.HBM)
    high, low, masks = kernel(
        functools.partial(split_kernel, bits),
        out_shape=[*pair, jax.ShapeDtypeStruct((2, 8, width), F32)],
        in_specs=[HBM] * 3,
        out_specs=[VMEM] * 3,
        scratch_shapes=[
            pltpu.SMEM(order.shape, jnp.int32),
            pltpu.SMEM(pattern.shape[1:], jnp.int32),
            pltpu.VMEM((rows, width), F32),
            pltpu.SemaphoreType.DMA((3,)),
        ],
        cost_estimate=cost(flops=4 * rows * width, bytes_accessed=8 * rows * width),
    )(held(order), held(pattern), held(own))
    near, high, low = kernel(
        functools.partial(near_kernel, bits),
        out_shape=[jax.ShapeDtypeStruct((BLOCK + HALF // 2, BLOCK), F32), *pair],
        in_specs=[VMEM] * 4,
        out_specs=[VMEM] * 3,
        cost_estimate=cost(flops=2 * flops, bytes_accessed=12 * rows * width),
    )(masks, high, low, sibling)
    near_sum = scanned(near, 0)
    far = kernel(
        far_kernel,
        out_shape=jax.ShapeDtypeStruct((rows, rows), F32),
        in_specs=[VMEM] * 4,
        out_specs=VMEM,
        cost_estimate=cost(flops=flops, bytes_accessed=8 * rows * width),
    )(masks, high, low, across)
    far_sum = scanned(far, 1)
    shared = moved(near_sum[HALF + HALF // 2 :], lambda p, r: (p, r ^ 1))
    theirs = moved(far_sum, lambda p, r: (p, r ^ 2 ^ odd(p, bits)))
    beside = moved(far_sum, lambda p, r: (p, r ^ 1))
    slots = targets.shape[0] * targets.shape[1]
    writing = cost(flops=0, bytes_accessed=12 * rows * panels.shape[1])
    begun, which = kernel(
        near_finish_kernel,
        out_shape=[jax.ShapeDtypeStruct(panels.shape, F32), jax.ShapeDtypeStruct((8, panels.shape[1]), jnp.int32)],
        in_specs=[SMEM] + [VMEM] * 3,
        out_specs=[VMEM] * 2,
        cost_estimate=writing,
    )(targets, panels, near_sum, shared)
    carried = kernel(
        functools.partial(far_finish_kernel, bits),
        out_shape=jax.ShapeDtypeStruct(panels.shape, F32),
        in_specs=[VMEM] * 5,
        out_specs=ANY,
        scratch_shapes=[pltpu.VMEM((slots, rows, BLOCK), F32), pltpu.SemaphoreType.DMA((slots,))],
        cost_estimate=writing,
    )(which, begun, far_sum, theirs, beside)
    return carried[None]


def solution(mesh):
    placed = (P("col", "row", None), P(), P(), P(), P("row", None))
    return jax.shard_map(
        body, mesh=mesh, in_specs=placed, out_specs=P("col", "row", None), check_vma=False
    )
```
